32 devices in a mesh: ctx: 8 (over y, x, core), mp: 4 (over z).
Axes of the slice: x: 2, y: 2, z: 4, core: 2. Of those that a mesh axis runs over, the one named last changes fastest.
Arguments:
- resid_in: bfloat16 [4096, 8192], P('ctx', 'mp'), may hold values from -6 to 6
- q_mr: bfloat16 [4096, 8192], P('ctx', 'mp'), may hold values from -6 to 6
- k_mr: bfloat16 [4096, 8192], P('ctx', 'mp'), may hold values from -6 to 6
- v_mr: bfloat16 [4096, 8192], P('ctx', 'mp'), may hold values from -6 to 6
- mr_filter: float32 [128, 8192], P(None, 'mp'), may hold values from -0.5 to 0.5
- mr_out: bfloat16 [8192, 8192], P('ctx', 'mp'), may hold values from -0.0625 to 0.0625
- q_li: bfloat16 [4096, 8192], P('ctx', 'mp'), may hold values from -6 to 6
- k_li: bfloat16 [4096, 8192], P('ctx', 'mp'), may hold values from -6 to 6
- li_rate: float32 [8192], P('mp'), may hold values from 2.4414063e-05 to 0.0333333333
- li_residue: float32 [8192], P('mp'), may hold values from 0.5 to 2
Outputs:
- mixed: bfloat16 [4096, 8192], P('ctx', 'mp')
- long_out: bfloat16 [4096, 8192], P('ctx', 'mp')
The draws below stay inside these ranges and needn't reach their ends.
All inputs are finite; a program needn't handle non-finite values.
Results may differ from the reference program's by a relative error of at most 0.008.
Values may be sent and summed in bfloat16 or wider, within the bound.
A program may use at most 192 MiB of HBM per device.

```python
import math
import jax
import jax.numpy as jnp
from jax import lax

D = 8192
TAPS = 128
SEQ = 4096


def draw_li_rate(key, part):
    key_mask, key_fast, key_slow = jax.random.split(key, 3)
    share = 0.5
    fast_mask = jax.random.uniform(key_mask, (D,)) < share
    fast = jax.random.uniform(key_fast, (D,), minval=1.0 / 50, maxval=1.0 / 30)
    slow = jnp.exp(jax.random.uniform(key_slow, (D,), minval=math.log(0.1 / SEQ), maxval=math.log(2.0 / SEQ)))
    return jnp.where(fast_mask, fast, slow).astype(jnp.float32)


def shard_levels(own_key, dims, pieces, least, top_value):
    factor_of = 1.0
    for dim, shards_of in pieces:
        heights = jax.random.uniform(jax.random.fold_in(jax.random.fold_in(own_key, 6), dim), (shards_of,), jnp.float32, least / len(pieces), top_value / len(pieces))
        factor_of = factor_of * jnp.repeat(jnp.exp(heights), dims[dim] // shards_of).reshape((-1,) + (1,) * (len(dims) - 1 - dim))
    return factor_of


def noise(rng, extent, spread, reach, cuts=(), dtype=jnp.bfloat16):
    loudness = shard_levels(rng, extent, cuts, -0.22, 0.18) if cuts else 1.0
    array = jax.random.normal(rng, extent, jnp.float32) * spread * loudness
    return jnp.minimum(jnp.maximum(array, -reach), reach).astype(dtype)


def setup_inputs(seed: int = 0) -> dict:
    key_list = jax.random.split(jax.random.key(seed), 11)
    return {
        "resid_in": noise(key_list[0], (SEQ, D), 1.0, 6.0, ((0, 8), (1, 4))),
        "q_mr": noise(key_list[1], (SEQ, D), 1.0, 6.0, ((0, 8), (1, 4))),
        "k_mr": noise(key_list[2], (SEQ, D), 1.0, 6.0, ((0, 8), (1, 4))),
        "v_mr": noise(key_list[3], (SEQ, D), 1.0, 6.0, ((0, 8), (1, 4))),
        "mr_filter": noise(key_list[4], (TAPS, D), TAPS ** -0.5, 0.5, ((1, 4),), jnp.float32),
        "mr_out": noise(key_list[5], (D, D), D ** -0.5, 0.0625, ((0, 8), (1, 4))),
        "q_li": noise(key_list[6], (SEQ, D), 1.0, 6.0, ((0, 8), (1, 4))),
        "k_li": noise(key_list[7], (SEQ, D), 1.0, 6.0, ((0, 8), (1, 4))),
        "li_rate": draw_li_rate(jax.random.fold_in(key_list[10], 71), 0),
        "li_residue": jnp.clip(0.5 + 1.5 * jax.random.uniform(key_list[9], (D,), jnp.float32) ** shard_levels(key_list[9], (D,), ((0, 4),), -0.2, 0.2), 0.5, 2.0),
    }


def reference(resid_in, q_mr, k_mr, v_mr, mr_filter, mr_out, q_li, k_li, li_rate, li_residue):
    drive_mr = (k_mr.astype(jnp.float32) * v_mr.astype(jnp.float32)).astype(jnp.bfloat16)
    padded = jnp.concatenate([jnp.zeros((TAPS - 1, D), jnp.float32), drive_mr.astype(jnp.float32)], 0)

    def add_tap(tap, total):
        start = (TAPS - 1 - tap).astype(jnp.int32)
        return total + mr_filter[tap][None, :] * lax.dynamic_slice_in_dim(padded, start, SEQ, 0)
    filtered = lax.fori_loop(0, TAPS, add_tap, jnp.zeros((SEQ, D), jnp.float32))
    gated = (q_mr.astype(jnp.float32) * filtered).astype(jnp.bfloat16)
    summed = jnp.dot(gated, mr_out, preferred_element_type=jnp.float32)
    mixed = (resid_in.astype(jnp.float32) + summed).astype(jnp.bfloat16)
    decay = jnp.exp(-li_rate)
    drive_li = k_li.astype(jnp.float32) * mixed.astype(jnp.float32)

    def advance(carry, row_in):
        carry = decay * carry + row_in
        return (carry, carry)
    _, state = lax.scan(advance, jnp.zeros((D,), jnp.float32), drive_li)
    scale = li_residue * jnp.sqrt(-jnp.expm1(-2.0 * li_rate))
    long_out = (q_li.astype(jnp.float32) * scale * state).astype(jnp.bfloat16)
    return (mixed, long_out)
```

```python
import functools

import jax
import jax.numpy as jnp
import numpy as np
from jax import lax
from jax.experimental import pallas as pl
from jax.experimental.pallas import tpu as pltpu
from jax.sharding import PartitionSpec as P

F32 = jnp.float32
BF16 = jnp.bfloat16
PIECE = 256
LANES = 512
BLOCK = 128
MESH = pl.DeviceIdType.MESH


def split(matrix):
    high = matrix.astype(BF16)
    low = (matrix - high.astype(np.float64)).astype(BF16)
    return np.concatenate([high, low], 0)


def transforms():
    size, half = 2 * BLOCK, BLOCK
    k = np.arange(half)[:, None]
    n = np.arange(size)[None, :]
    cos = np.cos(2 * np.pi * ((k * n) % size) / size)
    sin = -np.sin(2 * np.pi * ((k * n) % size) / size)
    nyquist = np.where(np.arange(size) % 2 == 0, 1.0, -1.0)
    forward_sin = sin.copy()
    forward_sin[0] = nyquist
    forward = np.concatenate([cos, forward_sin], 0)
    cos_nyquist = cos.copy()
    cos_nyquist[0] = nyquist
    of_filter = np.concatenate([cos, sin, cos_nyquist], 0)[:, :half]
    weight = np.where(k == 0, 1.0, 2.0) / size
    back_sin = sin * weight
    back_sin[0] = nyquist / size
    back = np.concatenate([cos * weight, back_sin], 0).T[half:]
    return split(forward), split(of_filter), split(back)


def mm(a, b):
    return jnp.dot(a, b, preferred_element_type=F32)


def mm2(stacked, b):
    rows = stacked.shape[0] // 2
    both = mm(stacked, b)
    return both[:rows] + both[rows:]


def w_plan(n, pieces):
    if n == 8 and pieces % 2 == 0:
        half = pieces // 2
        first, last = list(range(half)), list(range(half, pieces))
        own = []
        for a, b in zip(first + last, last + first):
            own += [(0, a, 2), (0, b, 4), (0, a, 1)]
        events = []
        for a, b in zip(first, last):
            events.append((2, a, [4, 1]))
            events.append((4, b, [2, 1]))
        for a, b in zip(last, first):
            events.append((2, a, [1]))
            events.append((4, b, [1]))
        for a, b in zip(first, last):
            events.append((6, a, [1]))
            events.append((6, b, [1]))
        tail = [(d, p) for d in (1, 3, 5, 7) for p in range(pieces)]
        return own, events, tail
    own = [(0, p, d) for d in range(1, n) for p in range(pieces)]
    return own, [], [(d, p) for d in range(1, n) for p in range(pieces)]


def kernel(
    n, m, pieces,
    resid_hbm, q_hbm, k_hbm, v_hbm, filt_hbm, w_hbm, qli_hbm, kli_hbm, rate_ref, scale_ref,
    fwd_ref, fil_ref, back_ref,
    mixed_hbm, long_hbm,
    kbuf, vbuf, qbuf, fbuf, halo, wbuf, gbuf, acc, ends, carry,
    lsem, wsend, wrecv, gsend, grecv, hsem, esend, erecv,
):
    rows, chans = kbuf.shape
    q_count = chans // LANES
    blocks = rows // BLOCK
    me = lax.axis_index("ctx")
    z = lax.axis_index("mp")

    def local(i, src, dst):
        return pltpu.make_async_copy(src, dst, lsem.at[i])

    load_k = local(0, k_hbm, kbuf)
    load_v = local(1, v_hbm, vbuf)
    load_q = local(2, q_hbm, qbuf)
    load_f = local(3, filt_hbm, fbuf)
    own_rows = pl.ds(pl.multiple_of(me * (pieces * PIECE), PIECE), pieces * PIECE)
    load_w = local(4, w_hbm, wbuf.at[own_rows])
    for copy in (load_k, load_v, load_f, load_q, load_w):
        copy.start()

    barrier = pltpu.get_barrier_semaphore()
    for d in range(1, n):
        pl.semaphore_signal(barrier, inc=1, device_id={"ctx": lax.rem(me + d, n)}, device_id_type=MESH)

    for d in range(1, m):
        pl.semaphore_signal(barrier, inc=1, device_id={"mp": lax.rem(z + d, m)}, device_id_type=MESH)
    pl.semaphore_wait(barrier, n + m - 2)

    def peer(d):
        return me + d - 2 * d_and(d) if n & (n - 1) == 0 else None

    def d_and(d):
        total = 0
        bit = 1
        while bit < n:
            if d & bit:
                total = total + bit * lax.rem(me // bit, 2)
            bit *= 2
        return total

    def piece_rows(d, p):
        return pl.ds(pl.multiple_of((peer(d) * pieces + p) * PIECE, PIECE), PIECE)

    sends = []

    def send_w(d, p, hop):
        src = w_hbm.at[pl.ds(p * PIECE, PIECE)] if d == 0 else wbuf.at[piece_rows(d, p)]
        copy = pltpu.make_async_remote_copy(
            src_ref=src,
            dst_ref=wbuf.at[piece_rows(d, p)],
            send_sem=wsend.at[len(sends)],
            recv_sem=wrecv.at[(d ^ hop) * pieces + p],
            device_id={"ctx": peer(hop)},
            device_id_type=MESH,
        )
        copy.start()
        sends.append(copy)

    def wait_w(d, p):
        pltpu.make_async_copy(
            wbuf.at[piece_rows(d, p)], wbuf.at[piece_rows(d, p)], wrecv.at[d * pieces + p]
        ).wait()

    own, events, tail = w_plan(n, pieces)
    for d, p, hop in own:
        send_w(d, p, hop)

    load_k.wait()
    load_v.wait()

    def drive_block(b, _):
        r = pl.ds(pl.multiple_of(b * BLOCK, BLOCK), BLOCK)
        kbuf[r] = (kbuf[r].astype(F32) * vbuf[r].astype(F32)).astype(BF16)
        return 0

    drive_block(blocks - 1, 0)
    halo_copy = pltpu.make_async_remote_copy(
        src_ref=kbuf.at[pl.ds(rows - BLOCK, BLOCK)],
        dst_ref=halo,
        send_sem=hsem.at[0],
        recv_sem=hsem.at[1],
        device_id={"ctx": lax.rem(me + 1, n)},
        device_id_type=MESH,
    )
    halo_copy.start()
    lax.fori_loop(0, blocks - 1, drive_block, 0)
    load_r = local(5, resid_hbm, vbuf)
    load_r.start()
    load_f.wait()
    load_q.wait()
    halo_copy.wait_recv()

    @pl.when(me == 0)
    def _():
        halo[...] = jnp.zeros_like(halo)

    def g_copy(up, k, j):
        source = z - k if up else z + k
        slot = source * q_count + j
        sem = ((0 if up else 1) * (m - 1) + k) * q_count + j
        return pltpu.make_async_remote_copy(
            src_ref=gbuf.at[slot],
            dst_ref=gbuf.at[slot],
            send_sem=gsend.at[sem],
            recv_sem=grecv.at[sem],
            device_id={"mp": z + 1 if up else z - 1},
            device_id_type=MESH,
        )

    def g_recv(up, k, j):
        source = z - 1 - k if up else z + 1 + k
        slot = source * q_count + j
        sem = ((0 if up else 1) * (m - 1) + k) * q_count + j
        pltpu.make_async_copy(gbuf.at[slot], gbuf.at[slot], grecv.at[sem]).wait()

    def conv(j, _):
        lanes = pl.ds(pl.multiple_of(j * LANES, LANES), LANES)
        taps = fbuf[:, lanes]
        high = taps.astype(BF16)
        low = (taps - high.astype(F32)).astype(BF16)
        spec = mm2(fil_ref[...], high) + mm(fil_ref[: 3 * BLOCK], low)
        a, b, c = spec[:BLOCK], spec[BLOCK : 2 * BLOCK], spec[2 * BLOCK :]
        for block in range(blocks - 1, -1, -1):
            if block == 0:
                window = jnp.concatenate([halo[:, lanes], kbuf[:BLOCK, lanes]], 0)
            else:
                window = kbuf[(block - 1) * BLOCK : (block + 1) * BLOCK, lanes]
            x = mm2(fwd_ref[...], window)
            xr, xi = x[:BLOCK], x[BLOCK:]
            y = jnp.concatenate([xr * a - xi * b, xr * b + xi * c], 0).astype(BF16)
            filtered = mm2(back_ref[...], y)
            r = slice(block * BLOCK, (block + 1) * BLOCK)
            gbuf[z * q_count + j, r] = (qbuf[r, lanes].astype(F32) * filtered).astype(BF16)

        @pl.when(z < m - 1)
        def _():
            g_copy(True, 0, j).start()

        @pl.when(z > 0)
        def _():
            g_copy(False, 0, j).start()

        return 0

    lax.fori_loop(0, q_count, conv, 0)
    halo_copy.wait_send()
    load_kl = local(6, kli_hbm, kbuf)
    load_kl.start()
    load_ql = local(7, qli_hbm, qbuf)
    load_ql.start()

    steps = [(k, j) for k in range(m - 1) for j in range(q_count)]
    done = 0
    for i, (k, j) in enumerate(steps):

        @pl.when(z - 1 - k >= 0)
        def _():
            g_recv(True, k, j)

            if k < m - 2:

                @pl.when(z < m - 1)
                def _():
                    g_copy(True, k + 1, j).start()

        @pl.when(z + 1 + k < m)
        def _():
            g_recv(False, k, j)

            if k < m - 2:

                @pl.when(z > 0)
                def _():
                    g_copy(False, k + 1, j).start()

        until = len(events) * (i + 1) // len(steps)
        for d, p, hops in events[done:until]:
            wait_w(d, p)
            for hop in hops:
                send_w(d, p, hop)
        done = until
    for d, p in tail:
        wait_w(d, p)
    load_w.wait()

    def multiply(step, _):
        g = step // (chans // LANES)
        cols = pl.ds(pl.multiple_of(lax.rem(step, chans // LANES) * LANES, LANES), LANES)
        part = mm(gbuf[g], wbuf[pl.ds(pl.multiple_of(g * LANES, LANES), LANES), cols])

        @pl.when(g == 0)
        def _():
            acc[:, cols] = part

        @pl.when(g > 0)
        def _():
            acc[:, cols] += part

        return 0

    lax.fori_loop(0, (m * q_count) * (chans // LANES), multiply, 0)
    load_r.wait()
    load_kl.wait()
    load_ql.wait()

    row = lax.broadcasted_iota(jnp.int32, (8, LANES), 0)

    def scan_lanes(j, _):
        lanes = pl.ds(pl.multiple_of(j * LANES, LANES), LANES)
        rate = jnp.broadcast_to(rate_ref[:, lanes], (8, LANES))
        power = jnp.exp(-rate * (row + 1).astype(F32))
        masked = [jnp.where(row >= s, jnp.exp(-rate * float(s)), 0.0) for s in (1, 2, 4)]

        def tile(t, last):
            r = pl.ds(pl.multiple_of(t * 16, 16), 16)
            value = (vbuf[r, lanes].astype(F32) + acc[r, lanes]).astype(BF16)
            vbuf[r, lanes] = value
            drive = kbuf[r, lanes].astype(F32) * value.astype(F32)
            out = []
            for h in range(2):
                x = drive[8 * h : 8 * h + 8]
                for s, coef in zip((1, 2, 4), masked):
                    x = x + coef * pltpu.roll(x, s, 0)
                x = x + power * last
                last = jnp.broadcast_to(x[7:8], (8, LANES))
                out.append(x)
            acc[r, lanes] = jnp.concatenate(out, 0)
            return last

        lax.fori_loop(0, rows // 16, tile, jnp.zeros((8, LANES), F32))
        return 0

    lax.fori_loop(0, chans // LANES, scan_lanes, 0)
    store_mixed = local(8, vbuf, mixed_hbm)
    store_mixed.start()

    def end_copy(d):
        return pltpu.make_async_remote_copy(
            src_ref=acc.at[pl.ds(rows - 8, 8)],
            dst_ref=ends.at[d],
            send_sem=esend.at[d],
            recv_sem=erecv.at[d],
            device_id={"ctx": lax.rem(me + d, n)},
            device_id_type=MESH,
        )

    for d in range(1, n):

        @pl.when(me + d < n)
        def _():
            end_copy(d).start()

    carry[...] = jnp.zeros_like(carry)
    jump = jnp.exp(-rate_ref[...] * float(rows))
    for d in range(n - 1, 0, -1):

        @pl.when(me >= d)
        def _():
            pltpu.make_async_copy(ends.at[d], ends.at[d], erecv.at[d]).wait()
            carry[...] = carry[...] * jump + ends[d, 7:8]

    def finish_lanes(j, _):
        lanes = pl.ds(pl.multiple_of(j * LANES, LANES), LANES)
        rate = jnp.broadcast_to(rate_ref[:, lanes], (8, LANES))
        scale = scale_ref[:, lanes]
        jump8 = jnp.exp(-rate * 8.0)
        first = carry[:, lanes] * jnp.exp(-rate * (row + 1).astype(F32))

        def tile(t, add):
            r = pl.ds(pl.multiple_of(t * 16, 16), 16)
            later = add * jump8
            state = acc[r, lanes] + jnp.concatenate([add, later], 0)
            qbuf[r, lanes] = (qbuf[r, lanes].astype(F32) * scale * state).astype(BF16)
            return later * jump8

        lax.fori_loop(0, rows // 16, tile, first)
        return 0

    lax.fori_loop(0, chans // LANES, finish_lanes, 0)
    store_long = local(9, qbuf, long_hbm)
    store_long.start()
    for copy in sends:
        copy.wait_send()
    for k, j in steps:

        @pl.when(jnp.logical_and(z - k >= 0, z < m - 1))
        def _():
            g_copy(True, k, j).wait_send()

        @pl.when(jnp.logical_and(z + k < m, z > 0))
        def _():
            g_copy(False, k, j).wait_send()

    for d in range(1, n):

        @pl.when(me + d < n)
        def _():
            end_copy(d).wait_send()

    store_mixed.wait()
    store_long.wait()


def body(n, m, resid_in, q_mr, k_mr, v_mr, mr_filter, mr_out, q_li, k_li, li_rate, li_residue):
    rows, chans = q_mr.shape
    taps = mr_filter.shape[0]
    assert taps == BLOCK
    pieces = mr_out.shape[0] // PIECE
    depth = mr_out.shape[0] * n
    q_count = chans // LANES
    forward, of_filter, back = (jnp.asarray(t) for t in transforms())
    own, events, _ = w_plan(n, pieces)
    send_count = len(own) + sum(len(hops) for _, _, hops in events)
    scale = li_residue * jnp.sqrt(-jnp.expm1(-2.0 * li_rate))
    hbm = pl.BlockSpec(memory_space=pl.ANY)
    vmem = pl.BlockSpec(memory_space=pltpu.VMEM)
    out = jax.ShapeDtypeStruct((rows, chans), BF16)
    dma = pltpu.SemaphoreType.DMA
    streams = 2 * (m - 1) * q_count
    return pl.pallas_call(
        functools.partial(kernel, n, m, pieces),
        out_shape=(out, out),
        in_specs=[hbm] * 8 + [vmem] * 5,
        out_specs=(hbm, hbm),
        scratch_shapes=[
            pltpu.VMEM((rows, chans), BF16),
            pltpu.VMEM((rows, chans), BF16),
            pltpu.VMEM((rows, chans), BF16),
            pltpu.VMEM((taps, chans), F32),
            pltpu.VMEM((BLOCK, chans), BF16),
            pltpu.VMEM((depth, chans), BF16),
            pltpu.VMEM((m * q_count, rows, LANES), BF16),
            pltpu.VMEM((rows, chans), F32),
            pltpu.VMEM((n, 8, chans), F32),
            pltpu.VMEM((8, chans), F32),
            dma((10,)),
            dma((send_count,)),
            dma((n * pieces,)),
            dma((streams,)),
            dma((streams,)),
            dma((2,)),
            dma((n,)),
            dma((n,)),
        ],
        compiler_params=pltpu.CompilerParams(
            collective_id=0, has_side_effects=True, vmem_limit_bytes=60 * 1024 * 1024
        ),
    )(
        resid_in, q_mr, k_mr, v_mr, mr_filter, mr_out, q_li, k_li,
        li_rate[None, :], scale[None, :], forward, of_filter, back,
    )


def solution(mesh):
    both = P("ctx", "mp")
    in_specs = (both, both, both, both, P(None, "mp"), both, both, both, P("mp"), P("mp"))
    fn = functools.partial(body, mesh.shape["ctx"], mesh.shape["mp"])
    return jax.shard_map(fn, mesh=mesh, in_specs=in_specs, out_specs=(both, both), check_vma=False)
```

```python
import functools

import jax
import jax.numpy as jnp
import numpy as np
from jax import lax
from jax.experimental import pallas as pl
from jax.experimental.pallas import tpu as pltpu
from jax.sharding import PartitionSpec as P

F32 = jnp.float32
BF16 = jnp.bfloat16
PIECE = 256
LANES = 512
BLOCK = 128
ORDER = [0, 0, 0, 0, 0, 0, 0, 8, 12, 12, 12, 12]
MESH = pl.DeviceIdType.MESH


def split(matrix):
    high = matrix.astype(BF16)
    low = (matrix - high.astype(np.float64)).astype(BF16)
    return np.concatenate([high, low], 0)


def transforms():
    size, half = 2 * BLOCK, BLOCK
    k = np.arange(half)[:, None]
    n = np.arange(size)[None, :]
    cos = np.cos(2 * np.pi * ((k * n) % size) / size)
    sin = -np.sin(2 * np.pi * ((k * n) % size) / size)
    nyquist = np.where(np.arange(size) % 2 == 0, 1.0, -1.0)
    forward_sin = sin.copy()
    forward_sin[0] = nyquist
    forward = np.concatenate([cos, forward_sin], 0)
    cos_nyquist = cos.copy()
    cos_nyquist[0] = nyquist
    of_filter = np.concatenate([cos, sin, cos_nyquist], 0)[:, :half]
    weight = np.where(k == 0, 1.0, 2.0) / size
    back_sin = sin * weight
    back_sin[0] = nyquist / size
    back = np.concatenate([cos * weight, back_sin], 0).T[half:]
    return split(forward), split(of_filter), split(back)


def mm(a, b):
    return jnp.dot(a, b, preferred_element_type=F32)


def mm2(stacked, b):
    rows = stacked.shape[0] // 2
    both = mm(stacked, b)
    return both[:rows] + both[rows:]


def w_plan(n, pieces):
    if n == 8 and pieces % 2 == 0:
        half = pieces // 2
        first, last = list(range(half)), list(range(half, pieces))
        own = []
        for a, b in zip(first + last, last + first):
            own += [(0, a, 2), (0, b, 4), (0, a, 1)]
        events = []
        for a, b in zip(first, last):
            events.append((2, a, [4, 1]))
            events.append((4, b, [2, 1]))
        for a, b in zip(last, first):
            events.append((2, a, [1]))
            events.append((4, b, [1]))
        for a, b in zip(first, last):
            events.append((6, a, [1]))
            events.append((6, b, [1]))
        tail = [(d, p) for d in (1, 3, 5, 7) for p in range(pieces)]
        return own, events, tail
    own = [(0, p, d) for d in range(1, n) for p in range(pieces)]
    return own, [], [(d, p) for d in range(1, n) for p in range(pieces)]


def kernel(
    n, m, pieces,
    resid_hbm, q_hbm, k_hbm, v_hbm, filt_hbm, w_hbm, qli_hbm, kli_hbm, rate_ref, scale_ref,
    fwd_ref, fil_ref, back_ref,
    mixed_hbm, long_hbm,
    kbuf, vbuf, qbuf, fbuf, halo, wbuf, gbuf, acc, ends, carry,
    lsem, wsend, wrecv, gsend, grecv, hsem, esend, erecv,
):
    rows, chans = kbuf.shape
    q_count = chans // LANES
    blocks = rows // BLOCK
    me = lax.axis_index("ctx")
    z = lax.axis_index("mp")

    def local(i, src, dst):
        return pltpu.make_async_copy(src, dst, lsem.at[i])

    load_k = local(0, k_hbm, kbuf)
    load_v = local(1, v_hbm, vbuf)
    load_q = local(2, q_hbm, qbuf)
    load_f = local(3, filt_hbm, fbuf)
    own_rows = pl.ds(pl.multiple_of(me * (pieces * PIECE), PIECE), pieces * PIECE)
    load_w = local(4, w_hbm, wbuf.at[own_rows])
    for copy in (load_k, load_v, load_f, load_q, load_w):
        copy.start()

    barrier = pltpu.get_barrier_semaphore()
    for d in range(1, n):
        pl.semaphore_signal(barrier, inc=1, device_id={"ctx": lax.rem(me + d, n)}, device_id_type=MESH)

    for d in range(1, m):
        pl.semaphore_signal(barrier, inc=1, device_id={"mp": lax.rem(z + d, m)}, device_id_type=MESH)
    pl.semaphore_wait(barrier, n + m - 2)

    def peer(d):
        return me + d - 2 * d_and(d) if n & (n - 1) == 0 else None

    def d_and(d):
        total = 0
        bit = 1
        while bit < n:
            if d & bit:
                total = total + bit * lax.rem(me // bit, 2)
            bit *= 2
        return total

    def piece_rows(d, p):
        return pl.ds(pl.multiple_of((peer(d) * pieces + p) * PIECE, PIECE), PIECE)

    sends = []

    def send_w(d, p, hop):
        src = w_hbm.at[pl.ds(p * PIECE, PIECE)] if d == 0 else wbuf.at[piece_rows(d, p)]
        copy = pltpu.make_async_remote_copy(
            src_ref=src,
            dst_ref=wbuf.at[piece_rows(d, p)],
            send_sem=wsend.at[len(sends)],
            recv_sem=wrecv.at[(d ^ hop) * pieces + p],
            device_id={"ctx": peer(hop)},
            device_id_type=MESH,
        )
        copy.start()
        sends.append(copy)

    def wait_w(d, p):
        pltpu.make_async_copy(
            wbuf.at[piece_rows(d, p)], wbuf.at[piece_rows(d, p)], wrecv.at[d * pieces + p]
        ).wait()

    own, events, tail = w_plan(n, pieces)
    for d, p, hop in own:
        send_w(d, p, hop)

    load_k.wait()
    load_v.wait()

    def drive_block(b, _):
        r = pl.ds(pl.multiple_of(b * BLOCK, BLOCK), BLOCK)
        kbuf[r] = (kbuf[r].astype(F32) * vbuf[r].astype(F32)).astype(BF16)
        return 0

    drive_block(blocks - 1, 0)
    halo_copy = pltpu.make_async_remote_copy(
        src_ref=kbuf.at[pl.ds(rows - BLOCK, BLOCK)],
        dst_ref=halo,
        send_sem=hsem.at[0],
        recv_sem=hsem.at[1],
        device_id={"ctx": lax.rem(me + 1, n)},
        device_id_type=MESH,
    )
    halo_copy.start()
    lax.fori_loop(0, blocks - 1, drive_block, 0)
    load_r = local(5, resid_hbm, vbuf)
    load_r.start()
    load_f.wait()
    load_q.wait()
    halo_copy.wait_recv()

    @pl.when(me == 0)
    def _():
        halo[...] = jnp.zeros_like(halo)

    def g_copy(up, k, j):
        source = z - k if up else z + k
        slot = source * q_count + j
        sem = ((0 if up else 1) * (m - 1) + k) * q_count + j
        return pltpu.make_async_remote_copy(
            src_ref=gbuf.at[slot],
            dst_ref=gbuf.at[slot],
            send_sem=gsend.at[sem],
            recv_sem=grecv.at[sem],
            device_id={"mp": z + 1 if up else z - 1},
            device_id_type=MESH,
        )

    def g_recv(up, k, j):
        source = z - 1 - k if up else z + 1 + k
        slot = source * q_count + j
        sem = ((0 if up else 1) * (m - 1) + k) * q_count + j
        pltpu.make_async_copy(gbuf.at[slot], gbuf.at[slot], grecv.at[sem]).wait()

    def conv(j, _):
        lanes = pl.ds(pl.multiple_of(j * LANES, LANES), LANES)
        taps = fbuf[:, lanes]
        high = taps.astype(BF16)
        low = (taps - high.astype(F32)).astype(BF16)
        spec = mm2(fil_ref[...], high) + mm(fil_ref[: 3 * BLOCK], low)
        a, b, c = spec[:BLOCK], spec[BLOCK : 2 * BLOCK], spec[2 * BLOCK :]
        for block in range(blocks - 1, -1, -1):
            if block == 0:
                window = jnp.concatenate([halo[:, lanes], kbuf[:BLOCK, lanes]], 0)
            else:
                window = kbuf[(block - 1) * BLOCK : (block + 1) * BLOCK, lanes]
            x = mm2(fwd_ref[...], window)
            xr, xi = x[:BLOCK], x[BLOCK:]
            y = jnp.concatenate([xr * a - xi * b, xr * b + xi * c], 0).astype(BF16)
            filtered = mm2(back_ref[...], y)
            r = slice(block * BLOCK, (block + 1) * BLOCK)
            gbuf[z * q_count + j, r] = (qbuf[r, lanes].astype(F32) * filtered).astype(BF16)

        @pl.when(z < m - 1)
        def _():
            g_copy(True, 0, j).start()

        @pl.when(z > 0)
        def _():
            g_copy(False, 0, j).start()

        return 0

    lax.fori_loop(0, q_count, conv, 0)
    halo_copy.wait_send()
    load_kl = local(6, kli_hbm, kbuf)
    load_kl.start()
    load_ql = local(7, qli_hbm, qbuf)
    load_ql.start()

    def multiply_zone(zone):
        def multiply(step, _):
            cols = pl.ds(pl.multiple_of(step * LANES, LANES), LANES)
            total = acc[:, cols]
            for g in range(zone * q_count, (zone + 1) * q_count):
                total = total + mm(gbuf[g], wbuf[g * LANES : (g + 1) * LANES, cols])
            acc[:, cols] = total
            return 0

        lax.fori_loop(0, chans // LANES, multiply, 0)

    early = n == 8 and m == 4 and bool(events)

    def ready_early(zone):
        near = jnp.logical_and(zone >= z - 1, zone <= z + 1)
        return jnp.logical_and(near, me // 2 != 3 - zone)

    acc[...] = jnp.zeros_like(acc)
    steps = [(k, j) for k in range(m - 1) for j in range(q_count)]
    done = 0
    for i, (k, j) in enumerate(steps):

        @pl.when(z - 1 - k >= 0)
        def _():
            g_recv(True, k, j)

            if k < m - 2:

                @pl.when(z < m - 1)
                def _():
                    g_copy(True, k + 1, j).start()

        @pl.when(z + 1 + k < m)
        def _():
            g_recv(False, k, j)

            if k < m - 2:

                @pl.when(z > 0)
                def _():
                    g_copy(False, k + 1, j).start()

        until = ORDER[i] if early and len(steps) == 12 else len(events)
        for d, p, hops in events[done:until]:
            wait_w(d, p)
            for hop in hops:
                send_w(d, p, hop)
        done = until
        if early and i == 2 * q_count - 1:
            for d, p in tail:
                if d != 7:
                    wait_w(d, p)
            load_w.wait()
            for zone in range(m):
                pl.when(ready_early(zone))(functools.partial(multiply_zone, zone))
    for d, p in tail:
        if d == 7 or not early:
            wait_w(d, p)
    if not early:
        load_w.wait()
    for zone in range(m):
        if early:
            pl.when(jnp.logical_not(ready_early(zone)))(functools.partial(multiply_zone, zone))
        else:
            multiply_zone(zone)

    load_r.wait()
    load_kl.wait()
    load_ql.wait()

    row = lax.broadcasted_iota(jnp.int32, (8, LANES), 0)

    def scan_lanes(j, _):
        lanes = pl.ds(pl.multiple_of(j * LANES, LANES), LANES)
        rate = jnp.broadcast_to(rate_ref[:, lanes], (8, LANES))
        power = jnp.exp(-rate * (row + 1).astype(F32))
        masked = [jnp.where(row >= s, jnp.exp(-rate * float(s)), 0.0) for s in (1, 2, 4)]

        def tile(t, last):
            r = pl.ds(pl.multiple_of(t * 16, 16), 16)
            value = (vbuf[r, lanes].astype(F32) + acc[r, lanes]).astype(BF16)
            vbuf[r, lanes] = value
            drive = kbuf[r, lanes].astype(F32) * value.astype(F32)
            out = []
            for h in range(2):
                x = drive[8 * h : 8 * h + 8]
                for s, coef in zip((1, 2, 4), masked):
                    x = x + coef * pltpu.roll(x, s, 0)
                x = x + power * last
                last = jnp.broadcast_to(x[7:8], (8, LANES))
                out.append(x)
            acc[r, lanes] = jnp.concatenate(out, 0)
            return last

        lax.fori_loop(0, rows // 16, tile, jnp.zeros((8, LANES), F32))
        return 0

    lax.fori_loop(0, chans // LANES, scan_lanes, 0)
    store_mixed = local(8, vbuf, mixed_hbm)
    store_mixed.start()

    def end_copy(d):
        return pltpu.make_async_remote_copy(
            src_ref=acc.at[pl.ds(rows - 8, 8)],
            dst_ref=ends.at[d],
            send_sem=esend.at[d],
            recv_sem=erecv.at[d],
            device_id={"ctx": lax.rem(me + d, n)},
            device_id_type=MESH,
        )

    for d in range(1, n):

        @pl.when(me + d < n)
        def _():
            end_copy(d).start()

    carry[...] = jnp.zeros_like(carry)
    jump = jnp.exp(-rate_ref[...] * float(rows))
    for d in range(n - 1, 0, -1):

        @pl.when(me >= d)
        def _():
            pltpu.make_async_copy(ends.at[d], ends.at[d], erecv.at[d]).wait()
            carry[...] = carry[...] * jump + ends[d, 7:8]

    def finish_lanes(j, _):
        lanes = pl.ds(pl.multiple_of(j * LANES, LANES), LANES)
        rate = jnp.broadcast_to(rate_ref[:, lanes], (8, LANES))
        scale = scale_ref[:, lanes]
        jump8 = jnp.exp(-rate * 8.0)
        first = carry[:, lanes] * jnp.exp(-rate * (row + 1).astype(F32))

        def tile(t, add):
            r = pl.ds(pl.multiple_of(t * 16, 16), 16)
            later = add * jump8
            state = acc[r, lanes] + jnp.concatenate([add, later], 0)
            qbuf[r, lanes] = (qbuf[r, lanes].astype(F32) * scale * state).astype(BF16)
            return later * jump8

        lax.fori_loop(0, rows // 16, tile, first)
        return 0

    lax.fori_loop(0, chans // LANES, finish_lanes, 0)
    store_long = local(9, qbuf, long_hbm)
    store_long.start()
    for copy in sends:
        copy.wait_send()
    for k, j in steps:

        @pl.when(jnp.logical_and(z - k >= 0, z < m - 1))
        def _():
            g_copy(True, k, j).wait_send()

        @pl.when(jnp.logical_and(z + k < m, z > 0))
        def _():
            g_copy(False, k, j).wait_send()

    for d in range(1, n):

        @pl.when(me + d < n)
        def _():
            end_copy(d).wait_send()

    store_mixed.wait()
    store_long.wait()


def body(n, m, resid_in, q_mr, k_mr, v_mr, mr_filter, mr_out, q_li, k_li, li_rate, li_residue):
    rows, chans = q_mr.shape
    taps = mr_filter.shape[0]
    assert taps == BLOCK
    pieces = mr_out.shape[0] // PIECE
    depth = mr_out.shape[0] * n
    q_count = chans // LANES
    forward, of_filter, back = (jnp.asarray(t) for t in transforms())
    own, events, _ = w_plan(n, pieces)
    send_count = len(own) + sum(len(hops) for _, _, hops in events)
    scale = li_residue * jnp.sqrt(-jnp.expm1(-2.0 * li_rate))
    hbm = pl.BlockSpec(memory_space=pl.ANY)
    vmem = pl.BlockSpec(memory_space=pltpu.VMEM)
    out = jax.ShapeDtypeStruct((rows, chans), BF16)
    dma = pltpu.SemaphoreType.DMA
    streams = 2 * (m - 1) * q_count
    return pl.pallas_call(
        functools.partial(kernel, n, m, pieces),
        out_shape=(out, out),
        in_specs=[hbm] * 8 + [vmem] * 5,
        out_specs=(hbm, hbm),
        scratch_shapes=[
            pltpu.VMEM((rows, chans), BF16),
            pltpu.VMEM((rows, chans), BF16),
            pltpu.VMEM((rows, chans), BF16),
            pltpu.VMEM((taps, chans), F32),
            pltpu.VMEM((BLOCK, chans), BF16),
            pltpu.VMEM((depth, chans), BF16),
            pltpu.VMEM((m * q_count, rows, LANES), BF16),
            pltpu.VMEM((rows, chans), F32),
            pltpu.VMEM((n, 8, chans), F32),
            pltpu.VMEM((8, chans), F32),
            dma((10,)),
            dma((send_count,)),
            dma((n * pieces,)),
            dma((streams,)),
            dma((streams,)),
            dma((2,)),
            dma((n,)),
            dma((n,)),
        ],
        compiler_params=pltpu.CompilerParams(
            collective_id=0, has_side_effects=True, vmem_limit_bytes=60 * 1024 * 1024
        ),
    )(
        resid_in, q_mr, k_mr, v_mr, mr_filter, mr_out, q_li, k_li,
        li_rate[None, :], scale[None, :], forward, of_filter, back,
    )


def solution(mesh):
    both = P("ctx", "mp")
    in_specs = (both, both, both, both, P(None, "mp"), both, both, both, P("mp"), P("mp"))
    fn = functools.partial(body, mesh.shape["ctx"], mesh.shape["mp"])
    return jax.shard_map(fn, mesh=mesh, in_specs=in_specs, out_specs=(both, both), check_vma=False)
```
